32 devices in a mesh: gx: 2 (over core), gy: 4 (over y, x), gz: 4 (over z).
Axes of the slice: x: 2, y: 2, z: 4, core: 2. Of those that a mesh axis runs over, the one named last changes fastest.
Arguments:
- displacement_start: float32 [3, 8, 64, 512], P(None, 'gx', 'gy', 'gz'), may hold values from -4 to 4
- external_force: float32 [3, 8, 64, 512], P(None, 'gx', 'gy', 'gz'), may hold values from -6 to 6
- damage_old: float32 [8, 64, 512], P('gx', 'gy', 'gz'), may hold values from 0 to 0.9
- history_old: float32 [8, 64, 512], P('gx', 'gy', 'gz'), may hold values from 0.02 to 2
- crack_labels: int32 [8, 64, 512], P('gx', 'gy', 'gz'), may hold values 0 or 1
- fixed_flags: int32 [8, 64, 512], P('gx', 'gy', 'gz'), may hold values 0 or 1
Outputs:
- displacement: float32 [3, 8, 64, 512], P(None, 'gx', 'gy', 'gz')
- damage: float32 [8, 64, 512], P('gx', 'gy', 'gz')
- history: float32 [8, 64, 512], P('gx', 'gy', 'gz')
The draws below stay inside these ranges and needn't reach their ends.
All inputs are finite; a program needn't handle non-finite values. No bound on the sum of `crack_labels` or of `fixed_flags` on one device may be relied on, other than what follows from the above.
Results may differ from the reference program's by a relative error of at most 0.0001.
Values sent between devices are 32-bit elements; how exact they have to be, the bound alone decides.
A program may use at most 64 MiB of HBM per device.

```python
import math
import jax
import jax.numpy as jnp
import numpy as np
from jax import lax

DISP_ITERS = 4
DMG_ITERS = 2
NX = 8
NY = 64
NZ = 512


def plant(array, key, least, top_value):
    shape = array.shape
    place = [jax.random.randint(jax.random.fold_in(key, axis), (), 0, shape[axis]) for axis in range(len(shape))]
    array = array.at[tuple(place)].set(least)
    longest = shape.index(max(shape))
    place[longest] = (place[longest] + 1) % shape[longest]
    return array.at[tuple(place)].set(top_value)


def block_scale(rng, dims, split, smallest, high):
    factor_of, own = 1.0, jax.random.fold_in(rng, 6)
    for axis_at, parts in split:
        steps = jnp.exp(jax.random.uniform(jax.random.fold_in(own, axis_at), (parts,), jnp.float32, smallest / len(split), high / len(split)))
        factor_of = factor_of * jnp.repeat(steps, dims[axis_at] // parts).reshape([-1 if axis == axis_at else 1 for axis in range(len(dims))])
    return factor_of


def noise(rng, dims, deviation, bound, shards=(), kind=jnp.bfloat16):
    level = block_scale(rng, dims, shards, -0.22, 0.18) if shards else 1.0
    array = jax.random.normal(rng, dims, jnp.float32) * deviation * level
    return jnp.minimum(jnp.maximum(array, -bound), bound).astype(kind)


def setup_inputs(seed: int = 0) -> dict:
    key_of = jax.random.split(jax.random.key(seed), 7)
    displacement_start = noise(key_of[0], (3, NX, NY, NZ), 0.5, 4.0, ((1, 2), (2, 4), (3, 4)), jnp.float32)
    external_force = noise(key_of[1], (3, NX, NY, NZ), 1.0, 6.0, ((1, 2), (2, 4), (3, 4)), jnp.float32)
    damage_old = jnp.clip(0.9 * jax.random.uniform(key_of[2], (NX, NY, NZ), jnp.float32) ** block_scale(key_of[2], (NX, NY, NZ), ((0, 2), (1, 4), (2, 4)), -0.2, 0.2), 0.0, 0.9)
    history_old = jnp.clip(jnp.exp(math.log(2.0) - 4.6051702 * jax.random.uniform(key_of[3], (NX, NY, NZ), jnp.float32) ** block_scale(key_of[3], (NX, NY, NZ), ((0, 2), (1, 4), (2, 4)), -0.2, 0.2)), 0.02, 2.0)
    crack_labels = plant((jax.random.randint(key_of[4], (NX, NY, NZ), 0, 32) < 1).astype(jnp.int32), jax.random.fold_in(key_of[4], 1), 0, 1)
    fixed_flags = plant((jax.random.randint(key_of[5], (NX, NY, NZ), 0, 16) < 1).astype(jnp.int32), jax.random.fold_in(key_of[5], 1), 0, 1)
    return dict(displacement_start=displacement_start, external_force=external_force, damage_old=damage_old, history_old=history_old, crack_labels=crack_labels, fixed_flags=fixed_flags)


LAME_LAMBDA = 0.5769230769230769
LAME_MU = 0.38461538461538464
BULK_MODULUS = LAME_LAMBDA + 2.0 * LAME_MU / 3.0
RESIDUAL_STIFFNESS = 0.001
TOUGHNESS = 1.0
LENGTH_SCALE = 2.0
CRACK_HISTORY = 40.0

def corner_offsets(corner):
    return (corner >> 2 & 1, corner >> 1 & 1, corner & 1)

def shape_gradients(sample):
    gradient = np.zeros((3, 8))
    for corner in range(8):
        offsets = corner_offsets(corner)
        values = [sample[k] if offsets[k] else 1.0 - sample[k] for k in range(3)]
        slopes = [1.0 if offsets[k] else -1.0 for k in range(3)]
        gradient[0, corner] = slopes[0] * values[1] * values[2]
        gradient[1, corner] = values[0] * slopes[1] * values[2]
        gradient[2, corner] = values[0] * values[1] * slopes[2]
    return gradient

def strain_matrix(gradient):
    strain = np.zeros((6, 24))
    for corner in range(8):
        column = 3 * corner
        strain[0, column] = gradient[0, corner]
        strain[1, column + 1] = gradient[1, corner]
        strain[2, column + 2] = gradient[2, corner]
        strain[3, column] = gradient[1, corner]
        strain[3, column + 1] = gradient[0, corner]
        strain[4, column + 1] = gradient[2, corner]
        strain[4, column + 2] = gradient[1, corner]
        strain[5, column] = gradient[2, corner]
        strain[5, column + 2] = gradient[0, corner]
    return strain

def element_tables():
    moduli = np.zeros((6, 6))
    moduli[:3, :3] = LAME_LAMBDA
    for k in range(3):
        moduli[k, k] += 2.0 * LAME_MU
        moduli[k + 3, k + 3] = LAME_MU
    points = [0.5 - 0.5 / np.sqrt(3.0), 0.5 + 0.5 / np.sqrt(3.0)]
    stiff_table = np.zeros((24, 24))
    laplace_table = np.zeros((8, 8))
    for sample_index in range(8):
        sample = tuple((points[k] for k in corner_offsets(sample_index)))
        gradient = shape_gradients(sample)
        strain = strain_matrix(gradient)
        stiff_table += 0.125 * strain.T @ moduli @ strain
        laplace_table += 0.125 * gradient.T @ gradient
    centre_table = strain_matrix(shape_gradients((0.5, 0.5, 0.5)))
    return (stiff_table.astype(np.float32), laplace_table.astype(np.float32), centre_table.astype(np.float32))

def corner_views(padded, element_shape):
    corner_list = []
    for corner in range(8):
        offx, offy, offz = corner_offsets(corner)
        corner_list.append(padded[..., offx:offx + element_shape[0], offy:offy + element_shape[1], offz:offz + element_shape[2]])
    return corner_list

def assemble_nodes(pieces):
    running = None
    for corner in range(8):
        offx, offy, offz = corner_offsets(corner)
        leading = [(0, 0)] * (pieces[corner].ndim - 3)
        placed = jnp.pad(pieces[corner], leading + [(offx, 1 - offx), (offy, 1 - offy), (offz, 1 - offz)])
        running = placed if running is None else running + placed
    return running

def valid_line(count):
    index = jnp.arange(count + 1, dtype=jnp.int32)
    return ((index >= 1) & (index <= count - 1)).astype(jnp.float32)

def strain_energy(strain):
    trace = strain[0] + strain[1] + strain[2]
    deviator = strain[:3] - trace[None] / 3.0
    shear = strain[3:]
    tensile = jnp.maximum(trace, 0.0)
    return 0.5 * BULK_MODULUS * tensile * tensile + LAME_MU * (lax.optimization_barrier(jnp.sum(deviator * deviator, axis=0)) + 0.5 * lax.optimization_barrier(jnp.sum(shear * shear, axis=0)))

def conjugate(solution, residual, apply_fn, inverse, count):
    precond = inverse * residual
    norm_now = jnp.sum(residual * precond)
    direction = precond
    for step in range(count):
        applied = apply_fn(direction)
        step_length = norm_now / jnp.sum(direction * applied)
        solution = solution + step_length * direction
        residual = residual - step_length * applied
        if step + 1 < count:
            precond = inverse * residual
            norm_next = jnp.sum(residual * precond)
            direction = precond + norm_next / norm_now * direction
            norm_now = norm_next
    return solution

def reference(displacement_start, external_force, damage_old, history_old, crack_labels, fixed_flags):
    tables = element_tables()
    stiff_table = jnp.asarray(tables[0], jnp.float32)
    laplace_table = jnp.asarray(tables[1], jnp.float32)
    centre_table = jnp.asarray(tables[2], jnp.float32)
    highest = lax.Precision.HIGHEST
    free_mask = 1.0 - fixed_flags.astype(jnp.float32)
    start_disp = displacement_start * free_mask[None]
    element_valid = valid_line(NX)[:, None, None] * valid_line(NY)[None, :, None] * valid_line(NZ)[None, None, :]
    element_shape = element_valid.shape
    damage_mean = sum(corner_views(jnp.pad(damage_old, 1), element_shape)) / 8.0
    stiffness = ((1.0 - damage_mean) ** 2 + RESIDUAL_STIFFNESS) * element_valid

    def elastic(nodal_field):
        padded = jnp.pad(nodal_field, ((0, 0), (1, 1), (1, 1), (1, 1)))
        corner_list = corner_views(padded, element_shape)
        pieces = []
        for target in range(8):
            running = None
            for source in range(8):
                block = stiff_table[3 * target:3 * target + 3, 3 * source:3 * source + 3]
                term = jnp.einsum('ij,jxyz->ixyz', block, corner_list[source], precision=highest)
                running = term if running is None else running + term
            pieces.append(stiffness[None] * running)
        return assemble_nodes(pieces)[:, 1:-1, 1:-1, 1:-1]

    def laplacian(nodal_field):
        corner_list = corner_views(jnp.pad(nodal_field, 1), element_shape)
        pieces = []
        for target in range(8):
            running = None
            for source in range(8):
                term = laplace_table[target, source] * corner_list[source]
                running = term if running is None else running + term
            pieces.append(element_valid * running)
        return assemble_nodes(pieces)[1:-1, 1:-1, 1:-1]
    disp_views = corner_views(jnp.pad(start_disp, ((0, 0), (1, 1), (1, 1), (1, 1))), element_shape)
    strain = None
    for source in range(8):
        term = jnp.einsum('ij,jxyz->ixyz', centre_table[:, 3 * source:3 * source + 3], disp_views[source], precision=highest)
        strain = term if strain is None else strain + term
    energy = strain_energy(strain) * element_valid
    nodal_energy = assemble_nodes([energy] * 8)[1:-1, 1:-1, 1:-1] / 8.0
    history = jnp.maximum(jnp.maximum(history_old, nodal_energy), CRACK_HISTORY * crack_labels.astype(jnp.float32))
    stiff_diag = jnp.diagonal(stiff_table)
    diag_pieces = [stiffness[None] * stiff_diag[3 * target:3 * target + 3][:, None, None, None] for target in range(8)]
    elastic_diag = assemble_nodes(diag_pieces)[:, 1:-1, 1:-1, 1:-1]
    inverse_elastic = 1.0 / (free_mask[None] * elastic_diag + (1.0 - free_mask[None]))

    def constrained(nodal_field):
        return free_mask[None] * elastic(free_mask[None] * nodal_field) + (1.0 - free_mask[None]) * nodal_field
    residual = free_mask[None] * (external_force - elastic(start_disp))
    displacement = conjugate(start_disp, residual, constrained, inverse_elastic, DISP_ITERS)
    reaction = TOUGHNESS / LENGTH_SCALE + 2.0 * history
    laplace_diag = assemble_nodes([element_valid * laplace_table[target, target] for target in range(8)])[1:-1, 1:-1, 1:-1]
    inverse_damage = 1.0 / (TOUGHNESS * LENGTH_SCALE * laplace_diag + reaction)

    def damage_operator(nodal_field):
        return TOUGHNESS * LENGTH_SCALE * laplacian(nodal_field) + reaction * nodal_field
    damage_residual = 2.0 * history - damage_operator(damage_old)
    damage = conjugate(damage_old, damage_residual, damage_operator, inverse_damage, DMG_ITERS)
    return (displacement, damage, history)
```

```python
import functools
import jax
import jax.numpy as jnp
import numpy as np
from jax import lax
from jax.experimental import pallas as pl
from jax.experimental.pallas import tpu as pltpu
from jax.sharding import PartitionSpec as P

DISP_ITERS = 4
DMG_ITERS = 2


LAME_LAMBDA = 0.5769230769230769
LAME_MU = 0.38461538461538464
BULK_MODULUS = LAME_LAMBDA + 2.0 * LAME_MU / 3.0
RESIDUAL_STIFFNESS = 0.001
TOUGHNESS = 1.0
LENGTH_SCALE = 2.0
CRACK_HISTORY = 40.0


def padded_2(cells, sides, width):
    for axis, dim in sides:
        count = lax.axis_size(axis)
        ends = count - 1
        head = lax.slice_in_dim(cells, 0, width, axis=dim)
        tail = lax.slice_in_dim(cells, cells.shape[dim] - width, cells.shape[dim], axis=dim)
        cells = jnp.concatenate(
            [
                lax.ppermute(tail, axis, [(i, (i + 1) % count) for i in range(ends)]),
                cells,
                lax.ppermute(head, axis, [((i + 1) % count, i) for i in range(ends)]),
            ],
            axis=dim,
        )
    return cells


def corner_offsets(corner):
    return (corner >> 2 & 1, corner >> 1 & 1, corner & 1)


def shape_gradients(sample):
    gradient = np.zeros((3, 8))
    for corner in range(8):
        offsets = corner_offsets(corner)
        values = [sample[k] if offsets[k] else 1.0 - sample[k] for k in range(3)]
        slopes = [1.0 if offsets[k] else -1.0 for k in range(3)]
        gradient[0, corner] = slopes[0] * values[1] * values[2]
        gradient[1, corner] = values[0] * slopes[1] * values[2]
        gradient[2, corner] = values[0] * values[1] * slopes[2]
    return gradient


def strain_matrix(gradient):
    strain = np.zeros((6, 24))
    for corner in range(8):
        column = 3 * corner
        strain[0, column] = gradient[0, corner]
        strain[1, column + 1] = gradient[1, corner]
        strain[2, column + 2] = gradient[2, corner]
        strain[3, column] = gradient[1, corner]
        strain[3, column + 1] = gradient[0, corner]
        strain[4, column + 1] = gradient[2, corner]
        strain[4, column + 2] = gradient[1, corner]
        strain[5, column] = gradient[2, corner]
        strain[5, column + 2] = gradient[0, corner]
    return strain


def element_tables():
    moduli = np.zeros((6, 6))
    moduli[:3, :3] = LAME_LAMBDA
    for k in range(3):
        moduli[k, k] += 2.0 * LAME_MU
        moduli[k + 3, k + 3] = LAME_MU
    points = [0.5 - 0.5 / np.sqrt(3.0), 0.5 + 0.5 / np.sqrt(3.0)]
    stiff_table = np.zeros((24, 24))
    laplace_table = np.zeros((8, 8))
    for sample_index in range(8):
        sample = tuple((points[k] for k in corner_offsets(sample_index)))
        gradient = shape_gradients(sample)
        strain = strain_matrix(gradient)
        stiff_table += 0.125 * strain.T @ moduli @ strain
        laplace_table += 0.125 * gradient.T @ gradient
    centre_table = strain_matrix(shape_gradients((0.5, 0.5, 0.5)))
    return (
        stiff_table.astype(np.float32),
        laplace_table.astype(np.float32),
        centre_table.astype(np.float32),
    )


def corner_views(padded, element_shape):
    corner_list = []
    for corner in range(8):
        offx, offy, offz = corner_offsets(corner)
        corner_list.append(
            padded[
                ...,
                offx : offx + element_shape[0],
                offy : offy + element_shape[1],
                offz : offz + element_shape[2],
            ]
        )
    return corner_list


def assemble_nodes(pieces):
    running = None
    for corner in range(8):
        offx, offy, offz = corner_offsets(corner)
        leading = [(0, 0)] * (pieces[corner].ndim - 3)
        placed = jnp.pad(
            pieces[corner], leading + [(offx, 1 - offx), (offy, 1 - offy), (offz, 1 - offz)]
        )
        running = placed if running is None else running + placed
    return running


def line_valid(position, devices, count):
    index = position * count + jnp.arange(count + 1, dtype=jnp.int32) - 1
    return ((index >= 0) & (index <= devices * count - 2)).astype(jnp.float32)


def strain_energy(strain):
    trace = strain[0] + strain[1] + strain[2]
    deviator = strain[:3] - trace[None] / 3.0
    shear = strain[3:]
    tensile = jnp.maximum(trace, 0.0)
    return 0.5 * BULK_MODULUS * tensile * tensile + LAME_MU * (
        jnp.sum(deviator * deviator, axis=0) + 0.5 * jnp.sum(shear * shear, axis=0)
    )


def forces_to_nodes(forces, stiffness):
    pieces = [stiffness[None] * forces[3 * target : 3 * target + 3] for target in range(8)]
    return assemble_nodes(pieces)


def element_apply(padded, stiffness, stiff_table):
    element_shape = stiffness.shape
    flat = jnp.stack(corner_views(padded, element_shape)).reshape(24, -1)
    forces = jnp.dot(stiff_table, flat, precision=lax.Precision.HIGHEST).reshape(
        (24,) + element_shape
    )
    return forces_to_nodes(forces, stiffness)


def laplace_apply(padded, element_valid, laplace_table):
    element_shape = element_valid.shape
    flat = jnp.stack(corner_views(padded, element_shape)).reshape(8, -1)
    forces = jnp.dot(laplace_table, flat, precision=lax.Precision.HIGHEST).reshape(
        (8,) + element_shape
    )
    return assemble_nodes([element_valid * forces[target] for target in range(8)])


def single_pair(pair):
    return tuple(lax.psum(pair, ("gx", "gy", "gz")))


def conjugate(solutions, residuals, inverses, counts, apply_fn):
    solutions = list(solutions)
    residuals = list(residuals)
    number = len(solutions)
    steps = max(counts)

    def pair_totals(pairs):
        return [single_pair(pairs[0])]

    precs = [inverses[0] * residuals[0]]
    applied = apply_fn(precs, list(range(number)))
    pairs = pair_totals([(jnp.sum(residuals[0] * precs[0]), jnp.sum(precs[0] * applied[0]))])
    norms = [pair[0] for pair in pairs]
    lengths = [pair[0] / pair[1] for pair in pairs]
    directions = list(precs)
    alongs = list(applied)
    for step in range(steps):
        active = [i for i in range(number) if step < counts[i]]
        for i in active:
            solutions[i] = solutions[i] + lengths[i] * directions[i]
            residuals[i] = residuals[i] - lengths[i] * alongs[i]
        later = [i for i in active if step + 1 < counts[i]]
        if later:
            i = later[0]
            precs[i] = inverses[i] * residuals[i]
            images = apply_fn([precs[i] for i in later], later)
            pairs = pair_totals(
                [
                    (jnp.sum(residuals[i] * precs[i]), jnp.sum(precs[i] * images[k]))
                    for k, i in enumerate(later)
                ]
            )
            for k, i in enumerate(later):
                norm_next, curve_sum = pairs[k]
                ratio = norm_next / norms[i]
                lengths[i] = norm_next / (curve_sum - ratio * norm_next / lengths[i])
                directions[i] = precs[i] + ratio * directions[i]
                alongs[i] = images[k] + ratio * alongs[i]
                norms[i] = norm_next
    return solutions


def body_any_mesh(displacement_start, external_force, damage_old, history_old, crack_labels, fixed_flags):
    tables = element_tables()
    stiff_table = jnp.asarray(tables[0], jnp.float32)
    laplace_table = jnp.asarray(tables[1], jnp.float32)
    centre_table = jnp.asarray(tables[2], jnp.float32)
    highest = lax.Precision.HIGHEST
    size_x, size_y, size_z = damage_old.shape
    free_mask = 1.0 - fixed_flags.astype(jnp.float32)
    start_disp = displacement_start * free_mask[None]
    element_valid = (
        line_valid(lax.axis_index("gx"), lax.axis_size("gx"), size_x)[:, None, None]
        * line_valid(lax.axis_index("gy"), lax.axis_size("gy"), size_y)[None, :, None]
        * line_valid(lax.axis_index("gz"), lax.axis_size("gz"), size_z)[None, None, :]
    )
    element_shape = element_valid.shape
    start_pad = padded_2(
        jnp.concatenate([start_disp, damage_old[None]], axis=0),
        (("gx", 1), ("gy", 2), ("gz", 3)),
        1,
    )
    corner_list = corner_views(start_pad, element_shape)
    damage_mean = sum((view[3] for view in corner_list)) / 8.0
    stiffness = ((1.0 - damage_mean) ** 2 + RESIDUAL_STIFFNESS) * element_valid
    flat = jnp.stack([view[:3] for view in corner_list]).reshape(24, -1)
    combined = jnp.dot(
        jnp.concatenate([stiff_table, centre_table], axis=0), flat, precision=highest
    )
    forces = combined[:24].reshape((24,) + element_shape)
    strain = combined[24:].reshape((6,) + element_shape)
    start_image = forces_to_nodes(forces, stiffness)[:, 1:-1, 1:-1, 1:-1]
    energy = strain_energy(strain) * element_valid
    nodal_energy = assemble_nodes([energy] * 8)[1:-1, 1:-1, 1:-1] / 8.0
    history = jnp.maximum(
        jnp.maximum(history_old, nodal_energy), CRACK_HISTORY * crack_labels.astype(jnp.float32)
    )
    stiff_diag = jnp.diagonal(stiff_table)
    diag_pieces = [
        stiffness[None] * stiff_diag[3 * target : 3 * target + 3][:, None, None, None]
        for target in range(8)
    ]
    elastic_diag = assemble_nodes(diag_pieces)[:, 1:-1, 1:-1, 1:-1]
    inverse_elastic = 1.0 / (free_mask[None] * elastic_diag + (1.0 - free_mask[None]))

    def constrained(nodal_field):
        masked = free_mask[None] * nodal_field
        padded = padded_2(masked, (("gx", 1), ("gy", 2), ("gz", 3)), 1)
        nodes = element_apply(padded, stiffness, stiff_table)[:, 1:-1, 1:-1, 1:-1]
        return free_mask[None] * nodes + (1.0 - free_mask[None]) * nodal_field

    reaction = TOUGHNESS / LENGTH_SCALE + 2.0 * history
    laplace_diag = assemble_nodes(
        [element_valid * laplace_table[target, target] for target in range(8)]
    )[1:-1, 1:-1, 1:-1]
    inverse_damage = 1.0 / (TOUGHNESS * LENGTH_SCALE * laplace_diag + reaction)
    residual = free_mask[None] * (external_force - start_image)
    start_lap = laplace_apply(start_pad[3], element_valid, laplace_table)[1:-1, 1:-1, 1:-1]
    damage_residual = 2.0 * history - (TOUGHNESS * LENGTH_SCALE * start_lap + reaction * damage_old)

    def damage_operator(nodal_field):
        padded = padded_2(nodal_field, (("gx", 0), ("gy", 1), ("gz", 2)), 1)
        lap_nodes = laplace_apply(padded, element_valid, laplace_table)[1:-1, 1:-1, 1:-1]
        return TOUGHNESS * LENGTH_SCALE * lap_nodes + reaction * nodal_field

    def single_elastic(fields, active):
        return [constrained(fields[0])]

    def single_damage(fields, active):
        return [damage_operator(fields[0])]

    displacement = conjugate(
        [start_disp], [residual], [inverse_elastic], [DISP_ITERS], single_elastic
    )[0]
    damage = conjugate(
        [damage_old], [damage_residual], [inverse_damage], [DMG_ITERS], single_damage
    )[0]
    return (displacement, damage, history)


DEPTH = 8
SPECTRUM = 3.2
MESH = pl.DeviceIdType.MESH


def walsh_tables():
    stiff, laplace, _ = element_tables()
    signs = np.array(
        [
            [np.prod([1.0 if c >> k & 1 else (-1.0 if m >> k & 1 else 1.0) for k in range(3)]) for c in range(8)]
            for m in range(8)
        ]
    )
    wide = np.kron(signs, np.eye(3))
    stiff_modes = wide @ stiff.astype(np.float64) @ wide.T / 64.0
    laplace_modes = signs @ laplace.astype(np.float64) @ signs.T / 64.0
    return stiff_modes, laplace_modes, float(stiff[0, 0]), float(laplace[0, 0])


def kernel(
    sizes,
    disp_ref,
    force_ref,
    damage_ref,
    history_ref,
    labels_ref,
    flags_ref,
    out_disp,
    out_damage,
    out_history,
    ext,
    modes,
    basis,
    resid,
    stiff,
    inverse,
    hist,
    dbasis,
    dresid,
    zsend,
    zrecv,
    zpart,
    sums,
    ysend_sem,
    yrecv_sem,
    zsend_sem,
    zrecv_sem,
    xsend_sem,
    xrecv_sem,
    asend_sem,
    arecv_sem,
):
    ngy, ngz, lx, ly, lz = sizes
    nx = 2 * lx
    rows, lanes = ly + 2 * DEPTH, lz + 128
    fields = 8
    npeer = ngy * ngz
    stiff_modes, laplace_modes, stiff_diag, laplace_diag = walsh_tables()
    gx, gy, gz = lax.axis_index("gx"), lax.axis_index("gy"), lax.axis_index("gz")
    xo = gx * lx
    other = 1 - gx
    me = gy * ngz + gz
    partner = (other, gy, gz)

    for p in range(lx):
        flag = flags_ref[p].astype(jnp.float32)
        free = 1.0 - flag
        for c in range(3):
            ext[c, xo + p, 0:ly, 0:lz] = free * disp_ref[c, p]
            ext[3 + c, xo + p, 0:ly, 0:lz] = force_ref[c, p]
        ext[6, xo + p, 0:ly, 0:lz] = damage_ref[p]
        top = jnp.maximum(history_ref[p], CRACK_HISTORY * labels_ref[p].astype(jnp.float32))
        ext[7, xo + p, 0:ly, 0:lz] = top * (free - flag)
        for f in range(fields):
            ext[f, xo + p, ly:rows, 0:lz] = jnp.zeros((2 * DEPTH, lz), jnp.float32)
    zrecv[...] = jnp.zeros_like(zrecv)

    barrier = pltpu.get_barrier_semaphore()
    pl.semaphore_signal(barrier, inc=1, device_id=partner, device_id_type=MESH)
    for o in range(1, npeer):
        q = lax.rem(me + o, npeer)
        pl.semaphore_signal(barrier, inc=1, device_id=(gx, q // ngz, lax.rem(q, ngz)), device_id_type=MESH)
    pl.semaphore_wait(barrier, npeer)

    own = pl.ds(xo, lx)

    def xcopy(src, dst, k):
        return pltpu.make_async_remote_copy(
            src_ref=src, dst_ref=dst, send_sem=xsend_sem.at[k], recv_sem=xrecv_sem.at[k],
            device_id=partner, device_id_type=MESH,
        )

    def ycopy(src_row, dst_row, k, shift):
        return pltpu.make_async_remote_copy(
            src_ref=ext.at[:, own, src_row : src_row + DEPTH, 0:lz],
            dst_ref=ext.at[:, own, dst_row : dst_row + DEPTH, 0:lz],
            send_sem=ysend_sem.at[k], recv_sem=yrecv_sem.at[k],
            device_id=(gx, gy + shift, gz), device_id_type=MESH,
        )

    def zcopy(k, shift):
        return pltpu.make_async_remote_copy(
            src_ref=zsend.at[k], dst_ref=zrecv.at[k],
            send_sem=zsend_sem.at[k], recv_sem=zrecv_sem.at[k],
            device_id=(gx, gy, gz + shift), device_id_type=MESH,
        )

    has_down, has_up = gy > 0, gy < ngy - 1
    has_left, has_right = gz > 0, gz < ngz - 1
    y_down = ycopy(0, ly, 0, -1)
    y_up = ycopy(ly - DEPTH, ly + DEPTH, 1, 1)
    x_own = xcopy(ext.at[:, own, 0:ly, 0:lz], ext.at[:, own, 0:ly, 0:lz], 0)
    pl.when(has_down)(y_down.start)
    pl.when(has_up)(y_up.start)
    x_own.start()
    pl.when(has_up)(y_down.wait_recv)
    pl.when(has_down)(y_up.wait_recv)

    x_ghost = xcopy(ext.at[:, own, ly:rows, 0:lz], ext.at[:, own, ly:rows, 0:lz], 1)
    x_ghost.start()
    group = lax.broadcasted_iota(jnp.int32, (rows, 128), 1) // 8
    count = fields * lx
    for j in range(count // 16):
        low = jnp.zeros((rows, 128), jnp.float32)
        high = jnp.zeros((rows, 128), jnp.float32)
        for k in range(16):
            f, p = divmod(16 * j + k, lx)
            first = ext[f, xo + p, :, 0:128]
            if lz == 128:
                turned = pltpu.roll(first, (8 * k + 8) % 128, 1) if k < 15 else first
                low = jnp.where(group == (k + 1) % 16, turned, low)
                high = jnp.where(group == k, turned, high)
        zsend[0, j] = low
        zsend[1, j] = high
    z_left = zcopy(0, -1)
    z_right = zcopy(1, 1)
    pl.when(has_left)(z_left.start)
    pl.when(has_right)(z_right.start)
    pl.when(has_right)(z_left.wait_recv)
    pl.when(has_left)(z_right.wait_recv)
    x_z = xcopy(zrecv, zpart, 2)
    x_z.start()

    def unpack(source, base):
        for j in range(count // 16):
            low = source[0, j]
            high = source[1, j]
            for k in range(16):
                f, p = divmod(16 * j + k, lx)
                both = jnp.where(group == k, high, jnp.where(group == (k + 1) % 16, low, 0.0))
                ext[f, base + p, :, lz : lz + 128] = (
                    pltpu.roll(both, (120 - 8 * k) % 128, 1) if k < 15 else both
                )

    unpack(zrecv, xo)
    x_own.wait_recv()
    x_ghost.wait_recv()
    x_z.wait_recv()
    unpack(zpart, other * lx)

    row = lax.broadcasted_iota(jnp.int32, (rows, lanes), 0)
    lane = lax.broadcasted_iota(jnp.int32, (rows, lanes), 1)
    ypos = gy * ly + jnp.where(row < ly + DEPTH, row, row - rows)
    zpos = gz * lz + jnp.where(lane < lz + 64, lane, lane - lanes)
    valid = jnp.where(
        (ypos >= 0) & (ypos <= ngy * ly - 2) & (zpos >= 0) & (zpos <= ngz * lz - 2), 1.0, 0.0
    )

    def up(a, axis):
        return pltpu.roll(a, a.shape[axis] - 1, axis)

    def down(a, axis):
        return pltpu.roll(a, 1, axis)

    def forward(u):
        near = up(u, 1)
        zs, zd = u + near, near - u
        a, b = up(zs, 0), up(zd, 0)
        return zs + a, a - zs, zd + b, b - zd

    def backward(ss, yd, zd, yz):
        s = (ss - yd) + down(ss + yd, 0)
        d = (zd - yz) + down(zd + yz, 0)
        return (s - d) + down(s + d, 1)

    def total8(a):
        s = a + up(a, 1)
        return s + up(s, 0)

    def total8_back(a):
        s = a + down(a, 1)
        return s + down(s, 0)

    def damage_sum(p):
        return total8(ext[6, p])

    def g_body(p, low):
        high = damage_sum(p + 1)
        rest = 1.0 - (low + high) * 0.125
        stiff[p] = (rest * rest + RESIDUAL_STIFFNESS) * valid
        return high

    lax.fori_loop(0, nx - 1, g_body, damage_sum(0))
    stiff[nx - 1] = jnp.zeros((rows, lanes), jnp.float32)

    def inv_body(p, low):
        here = total8_back(stiff[p])
        q = stiff_diag * (low + here)
        free = ext[7, p] > 0.0
        inverse[p] = jnp.where(free, 1.0 / jnp.where(free, q, 1.0), 0.0)
        return here

    lax.fori_loop(0, nx, inv_body, jnp.zeros((rows, lanes), jnp.float32))

    def pass_one(load, number):
        def step(p, carry):
            for c in range(number):
                out = forward(load(c, p))
                for m in range(4):
                    modes[4 * c + m, p] = out[m]
            return carry

        lax.fori_loop(0, nx, step, 0)

    def sm(mode_a, comp_a, mode_b, comp_b):
        return float(stiff_modes[3 * mode_a + comp_a, 3 * mode_b + comp_b])

    k_lame = sm(4, 0, 2, 1)
    k_two = sm(4, 0, 4, 0) - k_lame
    k_shear = sm(2, 0, 2, 0)
    k_twist = sm(3, 0, 5, 1)
    k_bend = sm(3, 1, 3, 1)
    k_cross = sm(3, 1, 5, 0)
    k_last = sm(7, 0, 7, 0)

    def element_pass(with_energy):
        def step(chunk, carry):
            r = pl.ds(pl.multiple_of(chunk * 8, 8), 8)
            low = [modes[m, 0, r, :] for m in range(12)]
            held = [None] * 12
            for p in range(nx):
                acc = held
                if p < nx - 1:
                    high = [modes[m, p + 1, r, :] for m in range(12)]
                    S = [low[m] + high[m] if m % 4 else None for m in range(12)]
                    D = [high[m] - low[m] for m in range(12)]
                    g = stiff[p, r, :]
                    xX, xXY, xXZ, xXYZ = D[0:4]
                    yX, yXY, yXZ, yXYZ = D[4:8]
                    zX, zXY, zXZ, zXYZ = D[8:12]
                    _, xY, xZ, xYZ = S[0:4]
                    _, yY, yZ, yYZ = S[4:8]
                    _, zY, zZ, zYZ = S[8:12]
                    div = xX + yY + zZ
                    sxy, sxz, syz = xY + yX, xZ + zX, yZ + zY
                    if with_energy:
                        trace = 0.25 * div
                        tens = jnp.maximum(trace, 0.0)
                        third = trace / 3.0
                        ex, ey, ez = 0.25 * xX - third, 0.25 * yY - third, 0.25 * zZ - third
                        dev = ex * ex + ey * ey + ez * ez
                        she = (sxy * sxy + sxz * sxz + syz * syz) * 0.0625
                        energy = 0.5 * BULK_MODULUS * tens * tens + LAME_MU * (dev + 0.5 * she)
                        hist[p, r, :] = jnp.where(g > 0.0, energy, 0.0)
                    gl, g2, gs = k_lame * g, k_two * g, k_shear * g
                    gt, gb, gc, g3 = k_twist * g, k_bend * g, k_cross * g, k_last * g
                    pressure = gl * div
                    fxX, fyY, fzZ = pressure + g2 * xX, pressure + g2 * yY, pressure + g2 * zZ
                    txy, txz, tyz = gs * sxy, gs * sxz, gs * syz
                    tw = xYZ + yXZ + zXY
                    fxYZ, fyXZ, fzXY = gt * (xYZ + tw), gt * (yXZ + tw), gt * (zXY + tw)
                    fyYZ, fxXZ = gb * yYZ + gc * xXZ, gb * xXZ + gc * yYZ
                    fzYZ, fxXY = gb * zYZ + gc * xXY, gb * xXY + gc * zYZ
                    fyXY, fzXZ = gb * yXY + gc * zXZ, gb * zXZ + gc * yXY
                    FD = [
                        fxX, fxXY, fxXZ, g3 * xXYZ,
                        txy, fyXY, fyXZ, g3 * yXYZ,
                        txz, fzXY, fzXZ, g3 * zXYZ,
                    ]
                    FS = [
                        None, txy, txz, fxYZ,
                        None, fyY, tyz, fyYZ,
                        None, tyz, fzZ, fzYZ,
                    ]
                    acc = [(-FD[m]) if FS[m] is None else FS[m] - FD[m] for m in range(12)]
                    if p:
                        acc = [acc[m] + held[m] for m in range(12)]
                    held = [FD[m] if FS[m] is None else FS[m] + FD[m] for m in range(12)]
                    low = high
                for m in range(12):
                    modes[m, p, r, :] = acc[m]
            return carry

        lax.fori_loop(0, rows // 8, step, 0)

    def nodes(c, p):
        return backward(*(modes[4 * c + m, p] for m in range(4)))

    def fold(a):
        part = a[0:8, 0:128]
        for i in range(0, ly, 8):
            for k in range(0, lz, 128):
                if i or k:
                    part = part + a[i : i + 8, k : k + 128]
        return part

    zero = jnp.zeros((8, 128), jnp.float32)
    inner = (slice(0, ly), slice(0, lz))

    pass_one(lambda c, p: ext[c, p], 3)
    element_pass(True)

    def start_step(p, carry):
        dot = carry
        inv = inverse[p]
        for c in range(3):
            r = ext[3 + c, p] - nodes(c, p)
            v = inv * r
            basis[c, p] = v
            resid[c, p] = r[inner]
            dot = dot + fold((v * r)[inner])
        return dot

    vector = [lax.fori_loop(0, nx, start_step, zero)]
    hist[nx - 1] = jnp.zeros((rows, lanes), jnp.float32)

    def hist_step(p, low):
        here = total8_back(hist[p])
        hist[p] = jnp.maximum(jnp.abs(ext[7, p]), 0.125 * (low + here))
        return here

    lax.fori_loop(0, nx, hist_step, jnp.zeros((rows, lanes), jnp.float32))

    gram = []
    for k in range(DISP_ITERS):
        pass_one(lambda c, p, k=k: basis[3 * k + c, p], 3)
        element_pass(False)
        more = k + 1 < DISP_ITERS

        def apply_step(p, carry, k=k, more=more):
            carry = list(carry)
            inv = inverse[p] * (2.0 / SPECTRUM) if more else None
            for c in range(3):
                w = nodes(c, p)
                wi = w[inner]
                for j in range(k + 1):
                    carry[j] = carry[j] + fold(basis[3 * j + c, p, 0:ly, 0:lz] * wi)
                if more:
                    v = inv * w - basis[3 * k + c, p]
                    if k:
                        v = 2.0 * v - basis[3 * (k - 1) + c, p] + 0.0
                    basis[3 * (k + 1) + c, p] = v
                    carry[k + 1] = carry[k + 1] + fold(v[inner] * resid[c, p])
            return tuple(carry)

        got = lax.fori_loop(0, nx, apply_step, (zero,) * (k + 1 + (1 if more else 0)))
        gram.append(list(got[: k + 1]))
        if more:
            vector.append(got[k + 1])

    l_one = float(laplace_modes[1, 1]) * TOUGHNESS * LENGTH_SCALE
    l_two = float(laplace_modes[3, 3]) * TOUGHNESS * LENGTH_SCALE
    l_three = float(laplace_modes[7, 7]) * TOUGHNESS * LENGTH_SCALE
    validrow = ((ypos >= 0) & (ypos <= ngy * ly - 2) & (zpos >= 0) & (zpos <= ngz * lz - 2))

    def laplace_pass(load):
        def prime(p):
            return forward(load(p))

        def step(p, carry):
            low, held = carry[:4], carry[4:]
            high = forward(load(p + 1))
            D = [high[m] - low[m] for m in range(4)]
            S = [low[m] + high[m] for m in range(1, 4)]
            F = [l_one * D[0], l_two * D[1], l_two * D[2], l_three * D[3]]
            F = [jnp.where(validrow, f, 0.0) for f in F]
            T = [l_one * S[0], l_one * S[1], l_two * S[2]]
            T = [jnp.where(validrow, f, 0.0) for f in T]
            acc = [-F[0], T[0] - F[1], T[1] - F[2], T[2] - F[3]]
            for m in range(4):
                modes[m, p] = acc[m] + held[m]
            return tuple(high) + (F[0], T[0] + F[1], T[1] + F[2], T[2] + F[3])

        blank = jnp.zeros((rows, lanes), jnp.float32)
        out = lax.fori_loop(0, nx - 1, step, tuple(prime(0)) + (blank,) * 4)
        for m in range(4):
            modes[m, nx - 1] = out[4 + m]

    corners = total8_back(valid) * (laplace_diag * TOUGHNESS * LENGTH_SCALE)

    def reaction_of(p):
        return TOUGHNESS / LENGTH_SCALE + 2.0 * hist[p]

    def damage_inverse(p):
        twice = jnp.where((p > 0) & (p < nx - 1), 2.0, 1.0)
        return 1.0 / (corners * twice + reaction_of(p))

    laplace_pass(lambda p: ext[6, p])

    def dstart(p, dot):
        d = ext[6, p]
        r = 2.0 * hist[p] - (nodes(0, p) + reaction_of(p) * d)
        v = damage_inverse(p) * r
        dbasis[0, p] = v
        dresid[p] = r[inner]
        return dot + fold((v * r)[inner])

    dvector = [lax.fori_loop(0, nx, dstart, zero)]
    dgram = []
    for k in range(DMG_ITERS):
        laplace_pass(lambda p, k=k: dbasis[k, p])
        more = k + 1 < DMG_ITERS

        def dstep(p, carry, k=k, more=more):
            carry = list(carry)
            here = dbasis[k, p]
            w = nodes(0, p) + reaction_of(p) * here
            for j in range(k + 1):
                carry[j] = carry[j] + fold((dbasis[j, p] * w)[inner])
            if more:
                v = damage_inverse(p) * w - here
                if k:
                    v = 2.0 * v - dbasis[k - 1, p]
                dbasis[k + 1, p] = v
                carry[k + 1] = carry[k + 1] + fold(v[inner] * dresid[p])
            return tuple(carry)

        got = lax.fori_loop(0, nx, dstep, (zero,) * (k + 1 + (1 if more else 0)))
        dgram.append(list(got[: k + 1]))
        if more:
            dvector.append(got[k + 1])

    parts = vector + dvector + [x for g in gram for x in g] + [x for g in dgram for x in g]
    at = lax.broadcasted_iota(jnp.int32, (8, 128), 1)
    packed = zero
    for i, part in enumerate(parts):
        packed = jnp.where(at == i, jnp.sum(jnp.sum(part, axis=0, keepdims=True), axis=1, keepdims=True), packed)
    sums[me] = packed

    def peer_copy(o, slot):
        q = lax.rem(me + o, npeer)
        return pltpu.make_async_remote_copy(
            src_ref=sums.at[me], dst_ref=sums.at[slot],
            send_sem=asend_sem.at[o - 1], recv_sem=arecv_sem.at[o - 1],
            device_id=(gx, q // ngz, lax.rem(q, ngz)), device_id_type=MESH,
        )

    sends = [peer_copy(o, me) for o in range(1, npeer)]
    for s in sends:
        s.start()
    for p in range(lx):
        out_history[p] = hist[xo + p, 0:ly, 0:lz]
    for o in range(1, npeer):
        peer_copy(o, lax.rem(me + npeer - o, npeer)).wait_recv()
    whole = sums[0]
    for i in range(1, npeer):
        whole = whole + sums[i]

    values = [
        jnp.sum(jnp.where(at[0:1] == i, whole[0:1], 0.0), axis=1, keepdims=True)
        for i in range(len(parts))
    ]
    nd, ng = DISP_ITERS, DMG_ITERS

    def solve(rhs, lower):
        n = len(rhs)
        A = [[lower[max(i, j)][min(i, j)] for j in range(n)] for i in range(n)]
        b = list(rhs)
        for i in range(n):
            pivot = 1.0 / A[i][i]
            for r in range(i + 1, n):
                ratio = A[r][i] * pivot
                for c in range(i + 1, n):
                    A[r][c] = A[r][c] - ratio * A[i][c]
                b[r] = b[r] - ratio * b[i]
        out = [None] * n
        for i in reversed(range(n)):
            s = b[i]
            for j in range(i + 1, n):
                s = s - A[i][j] * out[j]
            out[i] = s / A[i][i]
        return out

    def triangle(flat, n):
        return [[flat[k * (k + 1) // 2 + j] for j in range(k + 1)] for k in range(n)]

    rest = values[nd + ng :]
    cut = nd * (nd + 1) // 2
    weights = solve(values[:nd], triangle(rest[:cut], nd))
    dweights = solve(values[nd : nd + ng], triangle(rest[cut:], ng))
    for p in range(lx):
        for c in range(3):
            x = ext[c, xo + p, 0:ly, 0:lz]
            for k in range(nd):
                x = x + weights[k] * basis[3 * k + c, xo + p, 0:ly, 0:lz]
            out_disp[c, p] = x
        d = ext[6, xo + p, 0:ly, 0:lz]
        for k in range(ng):
            d = d + dweights[k] * dbasis[k, xo + p, 0:ly, 0:lz]
        out_damage[p] = d

    pl.when(has_down)(y_down.wait_send)
    pl.when(has_up)(y_up.wait_send)
    pl.when(has_left)(z_left.wait_send)
    pl.when(has_right)(z_right.wait_send)
    x_own.wait_send()
    x_ghost.wait_send()
    x_z.wait_send()
    for s in sends:
        s.wait_send()


def body_fused(sizes, *arrays):
    ngy, ngz, lx, ly, lz = sizes
    nx, rows, lanes, fields = 2 * lx, ly + 2 * DEPTH, lz + 128, 8
    packs = fields * lx // 16
    npeer = ngy * ngz
    f32 = jnp.float32
    wide = (nx, rows, lanes)
    vmem = pl.BlockSpec(memory_space=pltpu.VMEM)
    dma = pltpu.SemaphoreType.DMA
    return pl.pallas_call(
        functools.partial(kernel, sizes),
        out_shape=(
            jax.ShapeDtypeStruct((3, lx, ly, lz), f32),
            jax.ShapeDtypeStruct((lx, ly, lz), f32),
            jax.ShapeDtypeStruct((lx, ly, lz), f32),
        ),
        in_specs=[vmem] * 6,
        out_specs=(vmem,) * 3,
        scratch_shapes=[
            pltpu.VMEM((fields,) + wide, f32),
            pltpu.VMEM((12,) + wide, f32),
            pltpu.VMEM((3 * DISP_ITERS,) + wide, f32),
            pltpu.VMEM((3, nx, ly, lz), f32),
            pltpu.VMEM(wide, f32),
            pltpu.VMEM(wide, f32),
            pltpu.VMEM(wide, f32),
            pltpu.VMEM((DMG_ITERS,) + wide, f32),
            pltpu.VMEM((nx, ly, lz), f32),
            pltpu.VMEM((2, packs, rows, 128), f32),
            pltpu.VMEM((2, packs, rows, 128), f32),
            pltpu.VMEM((2, packs, rows, 128), f32),
            pltpu.VMEM((npeer, 8, 128), f32),
            dma((2,)),
            dma((2,)),
            dma((2,)),
            dma((2,)),
            dma((3,)),
            dma((3,)),
            dma((npeer - 1,)),
            dma((npeer - 1,)),
        ],
        compiler_params=pltpu.CompilerParams(
            collective_id=0, has_side_effects=True, vmem_limit_bytes=60 * 1024 * 1024
        ),
    )(*arrays)


def solution(mesh):
    shape = dict(mesh.shape)

    def body(*arrays):
        lx, ly, lz = arrays[2].shape
        fits = shape["gx"] == 2 and shape["gy"] * shape["gz"] > 1
        fits = fits and lx % 2 == 0 and ly % 8 == 0 and lz == 128
        if fits:
            return body_fused((shape["gy"], shape["gz"], lx, ly, lz), *arrays)
        return body_any_mesh(*arrays)

    return jax.shard_map(
        body,
        mesh=mesh,
        in_specs=(
            P(None, "gx", "gy", "gz"),
            P(None, "gx", "gy", "gz"),
            P("gx", "gy", "gz"),
            P("gx", "gy", "gz"),
            P("gx", "gy", "gz"),
            P("gx", "gy", "gz"),
        ),
        out_specs=(P(None, "gx", "gy", "gz"), P("gx", "gy", "gz"), P("gx", "gy", "gz")),
        check_vma=False,
    )
```

```python
import functools
import jax
import jax.numpy as jnp
import numpy as np
from jax import lax
from jax.experimental import pallas as pl
from jax.experimental.pallas import tpu as pltpu
from jax.sharding import PartitionSpec as P

DISP_ITERS = 4
DMG_ITERS = 2


LAME_LAMBDA = 0.5769230769230769
LAME_MU = 0.38461538461538464
BULK_MODULUS = LAME_LAMBDA + 2.0 * LAME_MU / 3.0
RESIDUAL_STIFFNESS = 0.001
TOUGHNESS = 1.0
LENGTH_SCALE = 2.0
CRACK_HISTORY = 40.0


def padded_2(cells, sides, width):
    for axis, dim in sides:
        count = lax.axis_size(axis)
        ends = count - 1
        head = lax.slice_in_dim(cells, 0, width, axis=dim)
        tail = lax.slice_in_dim(cells, cells.shape[dim] - width, cells.shape[dim], axis=dim)
        cells = jnp.concatenate(
            [
                lax.ppermute(tail, axis, [(i, (i + 1) % count) for i in range(ends)]),
                cells,
                lax.ppermute(head, axis, [((i + 1) % count, i) for i in range(ends)]),
            ],
            axis=dim,
        )
    return cells


def corner_offsets(corner):
    return (corner >> 2 & 1, corner >> 1 & 1, corner & 1)


def shape_gradients(sample):
    gradient = np.zeros((3, 8))
    for corner in range(8):
        offsets = corner_offsets(corner)
        values = [sample[k] if offsets[k] else 1.0 - sample[k] for k in range(3)]
        slopes = [1.0 if offsets[k] else -1.0 for k in range(3)]
        gradient[0, corner] = slopes[0] * values[1] * values[2]
        gradient[1, corner] = values[0] * slopes[1] * values[2]
        gradient[2, corner] = values[0] * values[1] * slopes[2]
    return gradient


def strain_matrix(gradient):
    strain = np.zeros((6, 24))
    for corner in range(8):
        column = 3 * corner
        strain[0, column] = gradient[0, corner]
        strain[1, column + 1] = gradient[1, corner]
        strain[2, column + 2] = gradient[2, corner]
        strain[3, column] = gradient[1, corner]
        strain[3, column + 1] = gradient[0, corner]
        strain[4, column + 1] = gradient[2, corner]
        strain[4, column + 2] = gradient[1, corner]
        strain[5, column] = gradient[2, corner]
        strain[5, column + 2] = gradient[0, corner]
    return strain


def element_tables():
    moduli = np.zeros((6, 6))
    moduli[:3, :3] = LAME_LAMBDA
    for k in range(3):
        moduli[k, k] += 2.0 * LAME_MU
        moduli[k + 3, k + 3] = LAME_MU
    points = [0.5 - 0.5 / np.sqrt(3.0), 0.5 + 0.5 / np.sqrt(3.0)]
    stiff_table = np.zeros((24, 24))
    laplace_table = np.zeros((8, 8))
    for sample_index in range(8):
        sample = tuple((points[k] for k in corner_offsets(sample_index)))
        gradient = shape_gradients(sample)
        strain = strain_matrix(gradient)
        stiff_table += 0.125 * strain.T @ moduli @ strain
        laplace_table += 0.125 * gradient.T @ gradient
    centre_table = strain_matrix(shape_gradients((0.5, 0.5, 0.5)))
    return (
        stiff_table.astype(np.float32),
        laplace_table.astype(np.float32),
        centre_table.astype(np.float32),
    )


def corner_views(padded, element_shape):
    corner_list = []
    for corner in range(8):
        offx, offy, offz = corner_offsets(corner)
        corner_list.append(
            padded[
                ...,
                offx : offx + element_shape[0],
                offy : offy + element_shape[1],
                offz : offz + element_shape[2],
            ]
        )
    return corner_list


def assemble_nodes(pieces):
    running = None
    for corner in range(8):
        offx, offy, offz = corner_offsets(corner)
        leading = [(0, 0)] * (pieces[corner].ndim - 3)
        placed = jnp.pad(
            pieces[corner], leading + [(offx, 1 - offx), (offy, 1 - offy), (offz, 1 - offz)]
        )
        running = placed if running is None else running + placed
    return running


def line_valid(position, devices, count):
    index = position * count + jnp.arange(count + 1, dtype=jnp.int32) - 1
    return ((index >= 0) & (index <= devices * count - 2)).astype(jnp.float32)


def strain_energy(strain):
    trace = strain[0] + strain[1] + strain[2]
    deviator = strain[:3] - trace[None] / 3.0
    shear = strain[3:]
    tensile = jnp.maximum(trace, 0.0)
    return 0.5 * BULK_MODULUS * tensile * tensile + LAME_MU * (
        jnp.sum(deviator * deviator, axis=0) + 0.5 * jnp.sum(shear * shear, axis=0)
    )


def forces_to_nodes(forces, stiffness):
    pieces = [stiffness[None] * forces[3 * target : 3 * target + 3] for target in range(8)]
    return assemble_nodes(pieces)


def element_apply(padded, stiffness, stiff_table):
    element_shape = stiffness.shape
    flat = jnp.stack(corner_views(padded, element_shape)).reshape(24, -1)
    forces = jnp.dot(stiff_table, flat, precision=lax.Precision.HIGHEST).reshape(
        (24,) + element_shape
    )
    return forces_to_nodes(forces, stiffness)


def laplace_apply(padded, element_valid, laplace_table):
    element_shape = element_valid.shape
    flat = jnp.stack(corner_views(padded, element_shape)).reshape(8, -1)
    forces = jnp.dot(laplace_table, flat, precision=lax.Precision.HIGHEST).reshape(
        (8,) + element_shape
    )
    return assemble_nodes([element_valid * forces[target] for target in range(8)])


def single_pair(pair):
    return tuple(lax.psum(pair, ("gx", "gy", "gz")))


def conjugate(solutions, residuals, inverses, counts, apply_fn):
    solutions = list(solutions)
    residuals = list(residuals)
    number = len(solutions)
    steps = max(counts)

    def pair_totals(pairs):
        return [single_pair(pairs[0])]

    precs = [inverses[0] * residuals[0]]
    applied = apply_fn(precs, list(range(number)))
    pairs = pair_totals([(jnp.sum(residuals[0] * precs[0]), jnp.sum(precs[0] * applied[0]))])
    norms = [pair[0] for pair in pairs]
    lengths = [pair[0] / pair[1] for pair in pairs]
    directions = list(precs)
    alongs = list(applied)
    for step in range(steps):
        active = [i for i in range(number) if step < counts[i]]
        for i in active:
            solutions[i] = solutions[i] + lengths[i] * directions[i]
            residuals[i] = residuals[i] - lengths[i] * alongs[i]
        later = [i for i in active if step + 1 < counts[i]]
        if later:
            i = later[0]
            precs[i] = inverses[i] * residuals[i]
            images = apply_fn([precs[i] for i in later], later)
            pairs = pair_totals(
                [
                    (jnp.sum(residuals[i] * precs[i]), jnp.sum(precs[i] * images[k]))
                    for k, i in enumerate(later)
                ]
            )
            for k, i in enumerate(later):
                norm_next, curve_sum = pairs[k]
                ratio = norm_next / norms[i]
                lengths[i] = norm_next / (curve_sum - ratio * norm_next / lengths[i])
                directions[i] = precs[i] + ratio * directions[i]
                alongs[i] = images[k] + ratio * alongs[i]
                norms[i] = norm_next
    return solutions


def body_any_mesh(displacement_start, external_force, damage_old, history_old, crack_labels, fixed_flags):
    tables = element_tables()
    stiff_table = jnp.asarray(tables[0], jnp.float32)
    laplace_table = jnp.asarray(tables[1], jnp.float32)
    centre_table = jnp.asarray(tables[2], jnp.float32)
    highest = lax.Precision.HIGHEST
    size_x, size_y, size_z = damage_old.shape
    free_mask = 1.0 - fixed_flags.astype(jnp.float32)
    start_disp = displacement_start * free_mask[None]
    element_valid = (
        line_valid(lax.axis_index("gx"), lax.axis_size("gx"), size_x)[:, None, None]
        * line_valid(lax.axis_index("gy"), lax.axis_size("gy"), size_y)[None, :, None]
        * line_valid(lax.axis_index("gz"), lax.axis_size("gz"), size_z)[None, None, :]
    )
    element_shape = element_valid.shape
    start_pad = padded_2(
        jnp.concatenate([start_disp, damage_old[None]], axis=0),
        (("gx", 1), ("gy", 2), ("gz", 3)),
        1,
    )
    corner_list = corner_views(start_pad, element_shape)
    damage_mean = sum((view[3] for view in corner_list)) / 8.0
    stiffness = ((1.0 - damage_mean) ** 2 + RESIDUAL_STIFFNESS) * element_valid
    flat = jnp.stack([view[:3] for view in corner_list]).reshape(24, -1)
    combined = jnp.dot(
        jnp.concatenate([stiff_table, centre_table], axis=0), flat, precision=highest
    )
    forces = combined[:24].reshape((24,) + element_shape)
    strain = combined[24:].reshape((6,) + element_shape)
    start_image = forces_to_nodes(forces, stiffness)[:, 1:-1, 1:-1, 1:-1]
    energy = strain_energy(strain) * element_valid
    nodal_energy = assemble_nodes([energy] * 8)[1:-1, 1:-1, 1:-1] / 8.0
    history = jnp.maximum(
        jnp.maximum(history_old, nodal_energy), CRACK_HISTORY * crack_labels.astype(jnp.float32)
    )
    stiff_diag = jnp.diagonal(stiff_table)
    diag_pieces = [
        stiffness[None] * stiff_diag[3 * target : 3 * target + 3][:, None, None, None]
        for target in range(8)
    ]
    elastic_diag = assemble_nodes(diag_pieces)[:, 1:-1, 1:-1, 1:-1]
    inverse_elastic = 1.0 / (free_mask[None] * elastic_diag + (1.0 - free_mask[None]))

    def constrained(nodal_field):
        masked = free_mask[None] * nodal_field
        padded = padded_2(masked, (("gx", 1), ("gy", 2), ("gz", 3)), 1)
        nodes = element_apply(padded, stiffness, stiff_table)[:, 1:-1, 1:-1, 1:-1]
        return free_mask[None] * nodes + (1.0 - free_mask[None]) * nodal_field

    reaction = TOUGHNESS / LENGTH_SCALE + 2.0 * history
    laplace_diag = assemble_nodes(
        [element_valid * laplace_table[target, target] for target in range(8)]
    )[1:-1, 1:-1, 1:-1]
    inverse_damage = 1.0 / (TOUGHNESS * LENGTH_SCALE * laplace_diag + reaction)
    residual = free_mask[None] * (external_force - start_image)
    start_lap = laplace_apply(start_pad[3], element_valid, laplace_table)[1:-1, 1:-1, 1:-1]
    damage_residual = 2.0 * history - (TOUGHNESS * LENGTH_SCALE * start_lap + reaction * damage_old)

    def damage_operator(nodal_field):
        padded = padded_2(nodal_field, (("gx", 0), ("gy", 1), ("gz", 2)), 1)
        lap_nodes = laplace_apply(padded, element_valid, laplace_table)[1:-1, 1:-1, 1:-1]
        return TOUGHNESS * LENGTH_SCALE * lap_nodes + reaction * nodal_field

    def single_elastic(fields, active):
        return [constrained(fields[0])]

    def single_damage(fields, active):
        return [damage_operator(fields[0])]

    displacement = conjugate(
        [start_disp], [residual], [inverse_elastic], [DISP_ITERS], single_elastic
    )[0]
    damage = conjugate(
        [damage_old], [damage_residual], [inverse_damage], [DMG_ITERS], single_damage
    )[0]
    return (displacement, damage, history)


DEPTH = 8
SPECTRUM = 3.2
MESH = pl.DeviceIdType.MESH


def walsh_tables():
    stiff, laplace, _ = element_tables()
    signs = np.array(
        [
            [np.prod([1.0 if c >> k & 1 else (-1.0 if m >> k & 1 else 1.0) for k in range(3)]) for c in range(8)]
            for m in range(8)
        ]
    )
    wide = np.kron(signs, np.eye(3))
    stiff_modes = wide @ stiff.astype(np.float64) @ wide.T / 64.0
    laplace_modes = signs @ laplace.astype(np.float64) @ signs.T / 64.0
    return stiff_modes, laplace_modes, float(stiff[0, 0]), float(laplace[0, 0])


def kernel(
    sizes,
    disp_ref,
    force_ref,
    damage_ref,
    history_ref,
    labels_ref,
    flags_ref,
    out_disp,
    out_damage,
    out_history,
    ext,
    modes,
    basis,
    resid,
    stiff,
    inverse,
    hist,
    react,
    spread,
    dinverse,
    dbasis,
    dresid,
    zsend,
    zrecv,
    zpart,
    sums,
    ysend_sem,
    yrecv_sem,
    zsend_sem,
    zrecv_sem,
    xsend_sem,
    xrecv_sem,
    asend_sem,
    arecv_sem,
):
    ngy, ngz, lx, ly, lz = sizes
    nx = 2 * lx
    rows = ly + 2 * DEPTH
    fields = 8
    npeer = ngy * ngz
    count = fields * lx
    stiff_modes, laplace_modes, stiff_diag, laplace_diag = walsh_tables()
    gx, gy, gz = lax.axis_index("gx"), lax.axis_index("gy"), lax.axis_index("gz")
    xo = gx * lx
    other = 1 - gx
    me = gy * ngz + gz
    partner = (other, gy, gz)

    GZ = nx
    barrier = pltpu.get_barrier_semaphore()
    pl.semaphore_signal(barrier, inc=1, device_id=partner, device_id_type=MESH)
    for o in range(1, npeer):
        q = lax.rem(me + o, npeer)
        pl.semaphore_signal(barrier, inc=1, device_id=(gx, q // ngz, lax.rem(q, ngz)), device_id_type=MESH)

    for p in range(lx):
        flag = flags_ref[p].astype(jnp.float32)
        free = 1.0 - flag
        for c in range(3):
            ext[c, xo + p, 0:ly] = free * disp_ref[c, p]
            ext[3 + c, xo + p, 0:ly] = force_ref[c, p]
        ext[6, xo + p, 0:ly] = damage_ref[p]
        top = jnp.maximum(history_ref[p], CRACK_HISTORY * labels_ref[p].astype(jnp.float32))
        ext[7, xo + p, 0:ly] = top * (free - flag)
    pl.semaphore_wait(barrier, npeer)

    own = pl.ds(xo, lx)

    def xcopy(src, dst, k):
        return pltpu.make_async_remote_copy(
            src_ref=src, dst_ref=dst, send_sem=xsend_sem.at[k], recv_sem=xrecv_sem.at[k],
            device_id=partner, device_id_type=MESH,
        )

    def ycopy(src_row, dst_row, k, shift):
        return pltpu.make_async_remote_copy(
            src_ref=ext.at[:, own, src_row : src_row + DEPTH, 0:lz],
            dst_ref=ext.at[:, own, dst_row : dst_row + DEPTH, 0:lz],
            send_sem=ysend_sem.at[k], recv_sem=yrecv_sem.at[k],
            device_id=(gx, gy + shift, gz), device_id_type=MESH,
        )

    def zcopy(k, shift):
        return pltpu.make_async_remote_copy(
            src_ref=zsend.at[k], dst_ref=zrecv.at[k],
            send_sem=zsend_sem.at[k], recv_sem=zrecv_sem.at[k],
            device_id=(gx, gy, gz + shift), device_id_type=MESH,
        )

    has_down, has_up = gy > 0, gy < ngy - 1
    has_left, has_right = gz > 0, gz < ngz - 1
    send_down = ycopy(0, ly, 0, -1)
    send_up = ycopy(ly - DEPTH, ly + DEPTH, 1, 1)
    x_own = xcopy(ext.at[:, own, 0:ly, 0:lz], ext.at[:, own, 0:ly, 0:lz], 0)
    pl.when(has_down)(send_down.start)
    pl.when(has_up)(send_up.start)
    x_own.start()

    @pl.when(jnp.logical_not(has_up))
    def _():
        for p in range(lx):
            for f in range(fields):
                ext[f, xo + p, ly : ly + DEPTH] = jnp.zeros((DEPTH, lz), jnp.float32)

    @pl.when(jnp.logical_not(has_down))
    def _():
        for p in range(lx):
            for f in range(fields):
                ext[f, xo + p, ly + DEPTH : rows] = jnp.zeros((DEPTH, lz), jnp.float32)

    @pl.when(jnp.logical_not(has_right))
    def _():
        zrecv[0] = jnp.zeros((count // 16, rows, 128), jnp.float32)

    @pl.when(jnp.logical_not(has_left))
    def _():
        zrecv[1] = jnp.zeros((count // 16, rows, 128), jnp.float32)

    pl.when(has_up)(send_down.wait_recv)
    pl.when(has_down)(send_up.wait_recv)

    x_ghost = xcopy(ext.at[:, own, ly:rows, 0:lz], ext.at[:, own, ly:rows, 0:lz], 1)
    x_ghost.start()
    group = lax.broadcasted_iota(jnp.int32, (rows, 128), 1) // 8
    for j in range(count // 16):
        low = jnp.zeros((rows, 128), jnp.float32)
        high = jnp.zeros((rows, 128), jnp.float32)
        for k in range(16):
            f, p = divmod(16 * j + k, lx)
            first = ext[f, xo + p, :, 0:128]
            turned = pltpu.roll(first, (8 * k + 8) % 128, 1) if k < 15 else first
            low = jnp.where(group == (k + 1) % 16, turned, low)
            high = jnp.where(group == k, turned, high)
        zsend[0, j] = low
        zsend[1, j] = high
    z_left = zcopy(0, -1)
    z_right = zcopy(1, 1)
    pl.when(has_left)(z_left.start)
    pl.when(has_right)(z_right.start)
    pl.when(has_right)(z_left.wait_recv)
    pl.when(has_left)(z_right.wait_recv)
    x_z = xcopy(zrecv, zpart, 2)
    x_z.start()

    def unpack(source, base, into, field):
        j = field * lx // 16
        low = source[0, j]
        high = source[1, j]
        for p in range(lx):
            k = field * lx + p - 16 * j
            both = jnp.where(group == k, high, low)
            turned = pltpu.roll(both, lax.rem(16 * base + (16 * p - 8 * k) % 128, 128), 1)
            into = jnp.where(group // 2 == base + p, turned, into)
        return into

    blank = jnp.zeros((rows, 128), jnp.float32)
    half = [unpack(zrecv, xo, blank, f) for f in range(fields)]
    for f in range(fields):
        ext[f, GZ] = half[f]
    x_own.wait_recv()
    x_ghost.wait_recv()
    x_z.wait_recv()
    for f in range(fields):
        ext[f, GZ] = unpack(zpart, other * lx, ext[f, GZ], f)

    row = lax.broadcasted_iota(jnp.int32, (rows, 128), 0)
    lane = lax.broadcasted_iota(jnp.int32, (rows, 128), 1)
    inside = lane % 16
    ypos = gy * ly + jnp.where(row < ly + DEPTH, row, row - rows)
    zpos = gz * lz + lane
    zghost = gz * lz + jnp.where(inside < 8, inside - 8, inside + (lz - 8))
    yvalid = (ypos >= 0) & (ypos <= ngy * ly - 2)
    valid = jnp.where(yvalid & (zpos <= ngz * lz - 2), 1.0, 0.0)
    gvalid = jnp.where(
        yvalid & (zghost >= 0) & (zghost <= ngz * lz - 2) & (lane < 16 * (nx - 1)), 1.0, 0.0
    )

    def y_up(a):
        return pltpu.roll(a, rows - 1, 0)

    def y_dn(a):
        return pltpu.roll(a, 1, 0)

    def z_up(a, ghost, p):
        return jnp.where(lane == 127, pltpu.roll(ghost, 119 - 16 * p, 1), pltpu.roll(a, 127, 1))

    def z_up_take(acc, a, p):
        return jnp.where(lane == 16 * p + 7, pltpu.roll(a, 16 * p + 7, 1), acc)

    def z_dn(a, ghost, p):
        return jnp.where(lane == 0, pltpu.roll(ghost, 121 - 16 * p, 1), pltpu.roll(a, 1, 1))

    def z_dn_take(acc, a, p):
        return jnp.where(lane == 16 * p + 8, pltpu.roll(a, 16 * p + 9, 1), acc)

    def x_up(a):
        return pltpu.roll(a, 112, 1)

    def x_dn(a):
        return pltpu.roll(a, 16, 1)

    def forward(u, near):
        zs, zd = u + near, near - u
        a, b = y_up(zs), y_up(zd)
        return zs + a, a - zs, zd + b, b - zd

    def half_back(ss, yd, zd, yz):
        s = (ss - yd) + y_dn(ss + yd)
        d = (zd - yz) + y_dn(zd + yz)
        return s - d, s + d

    def damage_sum(p):
        a = ext[6, p]
        s = a + z_up(a, ext[6, GZ], p)
        return s + y_up(s), a

    def rigidity(low, high, mask):
        rest = 1.0 - (low + high) * 0.125
        return (rest * rest + RESIDUAL_STIFFNESS) * mask

    def g_body(p, carry):
        low, ghost = carry
        high, a = damage_sum(p + 1)
        stiff[p] = rigidity(low, high, valid)
        return high, z_up_take(ghost, a, p + 1)

    sum_first, a_first = damage_sum(0)
    g_ghost = z_up_take(pltpu.roll(ext[6, GZ], 127, 1), a_first, 0)
    _, g_ghost = lax.fori_loop(0, nx - 1, g_body, (sum_first, g_ghost), unroll=True)
    g_ghost = ext[6, GZ] + g_ghost
    g_ghost = g_ghost + y_up(g_ghost)
    stiff[GZ] = rigidity(g_ghost, x_up(g_ghost), gvalid)
    stiff[nx - 1] = blank

    def gather_back(ref, emit):
        ghost = ref[GZ]

        def step(p, carry):
            low, taken = carry
            a = ref[p]
            s = a + z_dn(a, ghost, p)
            here = s + y_dn(s)
            emit(p, low + here)
            return here, z_dn_take(taken, a, p)

        _, taken = lax.fori_loop(0, nx, step, (blank, pltpu.roll(ghost, 1, 1)), unroll=True)
        s = ghost + taken
        s = s + y_dn(s)
        emit(GZ, s + x_dn(s))

    def inv_emit(p, total):
        q = stiff_diag * total
        free = ext[7, p] > 0.0
        inverse[p] = jnp.where(free, 1.0 / jnp.where(free, q, 1.0), 0.0)

    gather_back(stiff, inv_emit)

    def pass_one(load, number):
        ghosts = [load(c, GZ) for c in range(number)]

        def step(p, taken):
            new = []
            for c in range(number):
                u = load(c, p)
                out = forward(u, z_up(u, ghosts[c], p))
                for m in range(4):
                    modes[4 * c + m, p] = out[m]
                new.append(z_up_take(taken[c], u, p))
            return tuple(new)

        taken = lax.fori_loop(0, nx, step, tuple(pltpu.roll(g, 127, 1) for g in ghosts), unroll=True)
        for c in range(number):
            out = forward(ghosts[c], taken[c])
            for m in range(4):
                modes[4 * c + m, GZ] = out[m]

    def sm(mode_a, comp_a, mode_b, comp_b):
        return float(stiff_modes[3 * mode_a + comp_a, 3 * mode_b + comp_b])

    k_lame = sm(4, 0, 2, 1)
    k_two = sm(4, 0, 4, 0) - k_lame
    k_shear = sm(2, 0, 2, 0)
    k_twist = sm(3, 0, 5, 1)
    k_bend = sm(3, 1, 3, 1)
    k_cross = sm(3, 1, 5, 0)
    k_last = sm(7, 0, 7, 0)

    def element_pass(with_energy):
        def element(low, high, g, p, r):
            S = [low[m] + high[m] if m % 4 else None for m in range(12)]
            D = [high[m] - low[m] for m in range(12)]
            xX, xXY, xXZ, xXYZ = D[0:4]
            yX, yXY, yXZ, yXYZ = D[4:8]
            zX, zXY, zXZ, zXYZ = D[8:12]
            _, xY, xZ, xYZ = S[0:4]
            _, yY, yZ, yYZ = S[4:8]
            _, zY, zZ, zYZ = S[8:12]
            div = xX + yY + zZ
            sxy, sxz, syz = xY + yX, xZ + zX, yZ + zY
            if with_energy:
                trace = 0.25 * div
                tens = jnp.maximum(trace, 0.0)
                third = trace / 3.0
                ex, ey, ez = 0.25 * xX - third, 0.25 * yY - third, 0.25 * zZ - third
                dev = ex * ex + ey * ey + ez * ez
                she = (sxy * sxy + sxz * sxz + syz * syz) * 0.0625
                energy = 0.5 * BULK_MODULUS * tens * tens + LAME_MU * (dev + 0.5 * she)
                hist[p, r, :] = jnp.where(g > 0.0, energy, 0.0)
            gl, g2, gs = k_lame * g, k_two * g, k_shear * g
            gt, gb, gc, g3 = k_twist * g, k_bend * g, k_cross * g, k_last * g
            pressure = gl * div
            fxX, fyY, fzZ = pressure + g2 * xX, pressure + g2 * yY, pressure + g2 * zZ
            txy, txz, tyz = gs * sxy, gs * sxz, gs * syz
            tw = xYZ + yXZ + zXY
            fxYZ, fyXZ, fzXY = gt * (xYZ + tw), gt * (yXZ + tw), gt * (zXY + tw)
            fyYZ, fxXZ = gb * yYZ + gc * xXZ, gb * xXZ + gc * yYZ
            fzYZ, fxXY = gb * zYZ + gc * xXY, gb * xXY + gc * zYZ
            fyXY, fzXZ = gb * yXY + gc * zXZ, gb * zXZ + gc * yXY
            FD = [
                fxX, fxXY, fxXZ, g3 * xXYZ,
                txy, fyXY, fyXZ, g3 * yXYZ,
                txz, fzXY, fzXZ, g3 * zXYZ,
            ]
            FS = [
                None, txy, txz, fxYZ,
                None, fyY, tyz, fyYZ,
                None, tyz, fzZ, fzYZ,
            ]
            lows = [(-FD[m]) if FS[m] is None else FS[m] - FD[m] for m in range(12)]
            highs = [FD[m] if FS[m] is None else FS[m] + FD[m] for m in range(12)]
            return lows, highs

        def step(chunk, carry):
            r = pl.ds(pl.multiple_of(chunk * 8, 8), 8)
            low = [modes[m, 0, r, :] for m in range(12)]
            held = None
            for p in range(nx - 1):
                high = [modes[m, p + 1, r, :] for m in range(12)]
                lows, highs = element(low, high, stiff[p, r, :], p, r)
                for m in range(12):
                    modes[m, p, r, :] = lows[m] + held[m] if p else lows[m]
                held, low = highs, high
            for m in range(12):
                modes[m, nx - 1, r, :] = held[m]
            low = [modes[m, GZ, r, :] for m in range(12)]
            lows, highs = element(low, [x_up(a) for a in low], stiff[GZ, r, :], GZ, r)
            for m in range(12):
                modes[m, GZ, r, :] = lows[m] + x_dn(highs[m])
            return carry

        lax.fori_loop(0, rows // 8, step, 0, unroll=True)

    def each_node(number, emit, carry):
        ghosts = [half_back(*(modes[4 * c + m, GZ] for m in range(4))) for c in range(number)]

        def step(p, state):
            taken, carry = state
            new, values = [], []
            for c in range(number):
                near, far = half_back(*(modes[4 * c + m, p] for m in range(4)))
                values.append(near + z_dn(far, ghosts[c][1], p))
                new.append(z_dn_take(taken[c], far, p))
            return tuple(new), emit(p, values, carry, True)

        first = tuple(pltpu.roll(g[1], 1, 1) for g in ghosts)
        taken, carry = lax.fori_loop(0, nx, step, (first, carry), unroll=True)
        emit(GZ, [ghosts[c][0] + taken[c] for c in range(number)], carry, False)
        return carry

    def fold(a):
        part = a[0:8, 0:128]
        for i in range(0, ly, 8):
            for k in range(0, lz, 128):
                if i or k:
                    part = part + a[i : i + 8, k : k + 128]
        return part

    zero = jnp.zeros((8, 128), jnp.float32)
    inner = (slice(0, ly), slice(0, lz))

    pass_one(lambda c, p: ext[c, p], 3)
    element_pass(True)

    def start_emit(p, values, dot, main):
        inv = inverse[p]
        for c in range(3):
            r = ext[3 + c, p] - values[c]
            v = inv * r
            basis[c, p] = v
            if main:
                resid[c, p] = r[inner]
                dot = dot + fold((v * r)[inner])
        return dot

    vector = [each_node(3, start_emit, zero)]
    hist[nx - 1] = blank

    def hist_emit(p, total):
        react[p] = jnp.maximum(jnp.abs(ext[7, p]), 0.125 * total)

    gather_back(hist, hist_emit)

    gram = []
    for k in range(DISP_ITERS):
        pass_one(lambda c, p, k=k: basis[3 * k + c, p], 3)
        element_pass(False)
        more = k + 1 < DISP_ITERS

        def apply_emit(p, values, carry, main, k=k, more=more):
            carry = list(carry)
            if not main and not more:
                return tuple(carry)
            inv = inverse[p] * (2.0 / SPECTRUM) if more else None
            for c in range(3):
                w = values[c]
                if main:
                    wi = w[inner]
                    for j in range(k + 1):
                        carry[j] = carry[j] + fold(basis[3 * j + c, p, 0:ly] * wi)
                if more:
                    v = inv * w - basis[3 * k + c, p]
                    if k:
                        v = 2.0 * v - basis[3 * (k - 1) + c, p]
                    basis[3 * (k + 1) + c, p] = v
                    if main:
                        carry[k + 1] = carry[k + 1] + fold(v[inner] * resid[c, p])
            return tuple(carry)

        got = each_node(3, apply_emit, (zero,) * (k + 1 + (1 if more else 0)))
        gram.append(list(got[: k + 1]))
        if more:
            vector.append(got[k + 1])

    l_one = float(laplace_modes[1, 1]) * TOUGHNESS * LENGTH_SCALE
    l_two = float(laplace_modes[3, 3]) * TOUGHNESS * LENGTH_SCALE
    l_three = float(laplace_modes[7, 7]) * TOUGHNESS * LENGTH_SCALE

    def laplace_pass(load):
        pass_one(lambda c, p: load(p), 1)

        def element(low, high, mask):
            m1, m2, m3 = l_one * mask, l_two * mask, l_three * mask
            D = [high[m] - low[m] for m in range(4)]
            F = [m1 * D[0], m2 * D[1], m2 * D[2], m3 * D[3]]
            T = [m1 * (low[1] + high[1]), m1 * (low[2] + high[2]), m2 * (low[3] + high[3])]
            lows = [-F[0]] + [T[m] - F[m + 1] for m in range(3)]
            highs = [F[0]] + [T[m] + F[m + 1] for m in range(3)]
            return lows, highs

        for chunk in range(rows // 8):
            r = slice(8 * chunk, 8 * chunk + 8)
            low = [modes[m, 0, r, :] for m in range(4)]
            held = None
            for p in range(nx - 1):
                high = [modes[m, p + 1, r, :] for m in range(4)]
                lows, highs = element(low, high, valid[r])
                for m in range(4):
                    modes[m, p, r, :] = lows[m] + held[m] if p else lows[m]
                held, low = highs, high
            for m in range(4):
                modes[m, nx - 1, r, :] = held[m]
            low = [modes[m, GZ, r, :] for m in range(4)]
            lows, highs = element(low, [x_up(a) for a in low], gvalid[r])
            for m in range(4):
                modes[m, GZ, r, :] = lows[m] + x_dn(highs[m])

    spread[...] = jnp.zeros(spread.shape, jnp.float32)
    for p in range(nx - 1):
        spread[p] = valid
    spread[GZ] = gvalid

    def spread_emit(p, total):
        reaction = TOUGHNESS / LENGTH_SCALE + 2.0 * react[p]
        dinverse[p] = 1.0 / (total * (laplace_diag * TOUGHNESS * LENGTH_SCALE) + reaction)

    gather_back(spread, spread_emit)
    laplace_pass(lambda p: ext[6, p])

    def reaction_of(p):
        return TOUGHNESS / LENGTH_SCALE + 2.0 * react[p]

    def dstart(p, values, dot, main):
        r = 2.0 * react[p] - (values[0] + reaction_of(p) * ext[6, p])
        v = dinverse[p] * r
        dbasis[0, p] = v
        if main:
            dresid[p] = r[inner]
            dot = dot + fold((v * r)[inner])
        return dot

    dvector = [each_node(1, dstart, zero)]
    dgram = []
    for k in range(DMG_ITERS):
        laplace_pass(lambda p, k=k: dbasis[k, p])
        more = k + 1 < DMG_ITERS

        def dstep(p, values, carry, main, k=k, more=more):
            carry = list(carry)
            here = dbasis[k, p]
            w = values[0] + reaction_of(p) * here
            if main:
                for j in range(k + 1):
                    carry[j] = carry[j] + fold((dbasis[j, p] * w)[inner])
            if more:
                v = dinverse[p] * w - here
                if k:
                    v = 2.0 * v - dbasis[k - 1, p]
                dbasis[k + 1, p] = v
                if main:
                    carry[k + 1] = carry[k + 1] + fold(v[inner] * dresid[p])
            return tuple(carry)

        got = each_node(1, dstep, (zero,) * (k + 1 + (1 if more else 0)))
        dgram.append(list(got[: k + 1]))
        if more:
            dvector.append(got[k + 1])

    parts = vector + dvector + [x for g in gram for x in g] + [x for g in dgram for x in g]
    at = lax.broadcasted_iota(jnp.int32, (8, 128), 1)
    packed = zero
    for i, part in enumerate(parts):
        packed = jnp.where(at == i, jnp.sum(jnp.sum(part, axis=0, keepdims=True), axis=1, keepdims=True), packed)
    sums[me] = packed

    def peer_copy(o, slot):
        q = lax.rem(me + o, npeer)
        return pltpu.make_async_remote_copy(
            src_ref=sums.at[me], dst_ref=sums.at[slot],
            send_sem=asend_sem.at[o - 1], recv_sem=arecv_sem.at[o - 1],
            device_id=(gx, q // ngz, lax.rem(q, ngz)), device_id_type=MESH,
        )

    sends = [peer_copy(o, me) for o in range(1, npeer)]
    for s in sends:
        s.start()
    for p in range(lx):
        out_history[p] = react[xo + p, 0:ly]
    for o in range(1, npeer):
        peer_copy(o, lax.rem(me + npeer - o, npeer)).wait_recv()
    whole = sums[0]
    for i in range(1, npeer):
        whole = whole + sums[i]

    values = [
        jnp.sum(jnp.where(at[0:1] == i, whole[0:1], 0.0), axis=1, keepdims=True)
        for i in range(len(parts))
    ]
    nd, ng = DISP_ITERS, DMG_ITERS

    def solve(rhs, lower):
        n = len(rhs)
        A = [[lower[max(i, j)][min(i, j)] for j in range(n)] for i in range(n)]
        b = list(rhs)
        for i in range(n):
            pivot = 1.0 / A[i][i]
            for r in range(i + 1, n):
                ratio = A[r][i] * pivot
                for c in range(i + 1, n):
                    A[r][c] = A[r][c] - ratio * A[i][c]
                b[r] = b[r] - ratio * b[i]
        out = [None] * n
        for i in reversed(range(n)):
            s = b[i]
            for j in range(i + 1, n):
                s = s - A[i][j] * out[j]
            out[i] = s / A[i][i]
        return out

    def triangle(flat, n):
        return [[flat[k * (k + 1) // 2 + j] for j in range(k + 1)] for k in range(n)]

    rest = values[nd + ng :]
    cut = nd * (nd + 1) // 2
    weights = solve(values[:nd], triangle(rest[:cut], nd))
    dweights = solve(values[nd : nd + ng], triangle(rest[cut:], ng))
    for p in range(lx):
        for c in range(3):
            x = ext[c, xo + p, 0:ly, 0:lz]
            for k in range(nd):
                x = x + weights[k] * basis[3 * k + c, xo + p, 0:ly, 0:lz]
            out_disp[c, p] = x
        d = ext[6, xo + p, 0:ly, 0:lz]
        for k in range(ng):
            d = d + dweights[k] * dbasis[k, xo + p, 0:ly, 0:lz]
        out_damage[p] = d

    pl.when(has_down)(send_down.wait_send)
    pl.when(has_up)(send_up.wait_send)
    pl.when(has_left)(z_left.wait_send)
    pl.when(has_right)(z_right.wait_send)
    x_own.wait_send()
    x_ghost.wait_send()
    x_z.wait_send()
    for s in sends:
        s.wait_send()


def hand_on(*refs):
    for source, target in zip(refs[:3], refs[3:]):
        target[...] = source[...]


def body_fused(sizes, *arrays):
    ngy, ngz, lx, ly, lz = sizes
    nx, rows, fields = 2 * lx, ly + 2 * DEPTH, 8
    packs = fields * lx // 16
    npeer = ngy * ngz
    f32 = jnp.float32
    wide = (nx + 1, rows, lz)
    vmem = pl.BlockSpec(memory_space=pltpu.VMEM)
    dma = pltpu.SemaphoreType.DMA
    results = pl.pallas_call(
        functools.partial(kernel, sizes),
        out_shape=(
            jax.ShapeDtypeStruct((3, lx, ly, lz), f32),
            jax.ShapeDtypeStruct((lx, ly, lz), f32),
            jax.ShapeDtypeStruct((lx, ly, lz), f32),
        ),
        in_specs=[vmem] * 6,
        out_specs=(vmem,) * 3,
        scratch_shapes=[
            pltpu.VMEM((fields,) + wide, f32),
            pltpu.VMEM((12,) + wide, f32),
            pltpu.VMEM((3 * DISP_ITERS,) + wide, f32),
            pltpu.VMEM((3, nx, ly, lz), f32),
            pltpu.VMEM(wide, f32),
            pltpu.VMEM(wide, f32),
            pltpu.VMEM(wide, f32),
            pltpu.VMEM(wide, f32),
            pltpu.VMEM(wide, f32),
            pltpu.VMEM(wide, f32),
            pltpu.VMEM((DMG_ITERS,) + wide, f32),
            pltpu.VMEM((nx, ly, lz), f32),
            pltpu.VMEM((2, packs, rows, 128), f32),
            pltpu.VMEM((2, packs, rows, 128), f32),
            pltpu.VMEM((2, packs, rows, 128), f32),
            pltpu.VMEM((npeer, 8, 128), f32),
            dma((2,)),
            dma((2,)),
            dma((2,)),
            dma((2,)),
            dma((3,)),
            dma((3,)),
            dma((npeer - 1,)),
            dma((npeer - 1,)),
        ],
        compiler_params=pltpu.CompilerParams(
            collective_id=0, has_side_effects=True, vmem_limit_bytes=60 * 1024 * 1024
        ),
    )(*arrays)
    return pl.pallas_call(
        hand_on,
        out_shape=tuple(jax.ShapeDtypeStruct(r.shape, f32) for r in results),
        in_specs=[vmem] * 3,
        out_specs=(vmem,) * 3,
    )(*results)


def solution(mesh):
    shape = dict(mesh.shape)

    def body(*arrays):
        lx, ly, lz = arrays[2].shape
        fits = shape["gx"] == 2 and shape["gy"] * shape["gz"] > 1
        fits = fits and lx == 4 and ly % 8 == 0 and lz == 128
        if fits:
            return body_fused((shape["gy"], shape["gz"], lx, ly, lz), *arrays)
        return body_any_mesh(*arrays)

    return jax.shard_map(
        body,
        mesh=mesh,
        in_specs=(
            P(None, "gx", "gy", "gz"),
            P(None, "gx", "gy", "gz"),
            P("gx", "gy", "gz"),
            P("gx", "gy", "gz"),
            P("gx", "gy", "gz"),
            P("gx", "gy", "gz"),
        ),
        out_specs=(P(None, "gx", "gy", "gz"), P("gx", "gy", "gz"), P("gx", "gy", "gz")),
        check_vma=False,
    )
```
